512 devices in a mesh: dp: 4 (over x_hi, core), context: 16 (over x_lo, z), tensor: 8 (over y).
Axes of the slice: x: 4 (x_hi: 2, x_lo: 2; x = x_hi * 2 + x_lo), y: 8, z: 8, core: 2. Of those that a mesh axis runs over, the one named last changes fastest.
Arguments:
- tokens: bfloat16 [32768, 4096], P(('dp', 'context', 'tensor')), parts along dimension 0, may hold values from -6 to 6
- norm_gain: bfloat16 [4096], replicated, may hold values from 0.099609375 to 1.8984375
- w_query: bfloat16 [4096, 2048], P(None, 'tensor'), may hold values from -2.03125 to 2.03125
- key_matrix: bfloat16 [4096, 1024], P(None, 'tensor'), may hold values from -0.109375 to 0.109375
- value_matrix: bfloat16 [4096, 1024], P(None, 'tensor'), may hold values from -0.09375 to 0.09375
- seg_ids: int32 [32768], P('dp'), parts along dimension 0, may hold values from 0 to 7, never falling along the last dimension, each value on 1 to 4096 neighbouring positions
Outputs:
- attended: bfloat16 [32768, 2048], P(('dp', 'context'), 'tensor'), parts along dimension 0
The draws below stay inside these ranges and needn't reach their ends.
There are 4 independent parts, one for each index of `dp`. The reference program is written for one: setup_inputs(seed, part) draws one part's arguments, and reference() takes and returns one part's arrays. A program takes and returns all parts, laid end to end along the dimension named above; an argument that names none is the same for every part. Nothing has to cross between parts.
Inputs may be any that keep to these rules, and one draw needn't show every extreme that they name: `seg_ids`: never falls along the row; each of the 8 documents covers 1 to 4096 positions, one exactly 4096.
All inputs are finite; a program needn't handle non-finite values.
Results may differ from the reference program's by a relative error of at most 0.0078.
Values may be sent and summed in bfloat16 or wider, within the bound.
A program may use at most 64 MiB of HBM per device.

```python
import math
import jax
import jax.numpy as jnp
import numpy as np
from jax import lax

MODEL_WIDTH = 4096
LOCAL_QUERY_HEADS = 16
KEY_VALUE_HEADS = 8
HEAD_SIZE = 128
DOCS = 8
PACKED_TOKENS = 8192


def key_unrotated(key):
    unnormalized_rows = jax.random.normal(jax.random.fold_in(key, 11), (MODEL_WIDTH, KEY_VALUE_HEADS * HEAD_SIZE), jnp.float32)
    return jnp.clip(unnormalized_rows, -6.0, 6.0) / math.sqrt(MODEL_WIDTH)


def draw_key_matrix(key, part):
    return key_unrotated(key).astype(jnp.bfloat16)


def draw_w_query(key, part):
    unnormalized_rows = jax.random.normal(jax.random.fold_in(key, 23), (MODEL_WIDTH, LOCAL_QUERY_HEADS * HEAD_SIZE), jnp.float32)
    own_part = jnp.clip(unnormalized_rows, -6.0, 6.0) / math.sqrt(MODEL_WIDTH)
    return own_part.astype(jnp.bfloat16)


def block_levels(key, shape, pieces, low, high):
    factor_of = 1.0
    for position, blocks in pieces:
        draws = jax.random.uniform(jax.random.fold_in(jax.random.fold_in(key, 6), position), (blocks,), jnp.float32, low / len(pieces), high / len(pieces))
        factor_of = factor_of * jnp.repeat(jnp.exp(draws), shape[position] // blocks).reshape((-1,) + (1,) * (len(shape) - 1 - position))
    return factor_of


def length_profile(amount, total, bound, lean):
    loads = [(1 << 20) // math.isqrt(rank ** lean) + 1 for rank in range(2, amount + 1)]
    rest, given = total - bound - (amount - 1), [1] * (amount - 1)
    while rest > 0:
        candidates = [i for i in range(amount - 1) if given[i] < bound]
        whole, left = sum([loads[i] for i in candidates]), rest
        for i in candidates:
            addition = min(bound - given[i], max(1, left * loads[i] // whole), rest)
            given[i] = given[i] + addition
            rest = rest - addition
    return np.array([bound] + given)


def uneven(stream_key, amount, total, reach, lean):
    if amount == 2:
        one = jax.random.randint(stream_key, (), max(1, total - reach), min(reach, total - 1) + 1)
        return jnp.stack([one, total - one])
    lengths = jnp.asarray(length_profile(amount, total, reach, lean), jnp.int32)
    couples = (amount - 1) // 2
    donor, sink = lengths[1:1 + 2 * couples:2], lengths[2:2 + 2 * couples:2]
    room = jnp.minimum(donor - 1, reach - sink)
    passed = jax.random.randint(jax.random.fold_in(stream_key, 1), (couples,), 0, 1 << 20) % (room + 1)
    lengths = lengths.at[1:1 + 2 * couples:2].set(donor - passed).at[2:2 + 2 * couples:2].set(sink + passed)
    return lengths[jax.random.permutation(jax.random.fold_in(stream_key, 2), amount)]


def bell_draw(stream_key, dims, spread, limit, split=(), kind=jnp.bfloat16):
    array = spread * jax.random.normal(stream_key, dims, jnp.float32)
    if split:
        array = array * block_levels(stream_key, dims, split, -0.22, 0.18)
    return jnp.clip(array, -limit, limit).astype(kind)


def setup_inputs(seed: int = 0, part: int = 0) -> dict:
    key_of = jax.random.split(jax.random.key(seed), 7)
    part_splits = jax.random.split(jax.random.fold_in(key_of[6], part), 7)
    return {
        "tokens": bell_draw(part_splits[0], (PACKED_TOKENS, MODEL_WIDTH), 1.0, 6.0, ((0, 128),)),
        "norm_gain": jnp.clip(1.0 + 0.18 * jax.random.normal(key_of[1], (MODEL_WIDTH,), jnp.float32), 0.099609375, 1.8984375).astype(jnp.bfloat16),
        "w_query": draw_w_query(jax.random.fold_in(key_of[6], 71), part),
        "key_matrix": draw_key_matrix(jax.random.fold_in(key_of[6], 71), part),
        "value_matrix": bell_draw(key_of[4], (MODEL_WIDTH, KEY_VALUE_HEADS * HEAD_SIZE), MODEL_WIDTH ** -0.5, 0.09375, ((1, 8),)),
        "seg_ids": jnp.searchsorted(jnp.cumsum(uneven(part_splits[5], DOCS, PACKED_TOKENS, PACKED_TOKENS // 2, 1)), jnp.arange(PACKED_TOKENS), side="right").astype(jnp.int32),
    }


def rotate(vectors, positions):
    half_width = vectors.shape[-1] // 2
    inv_freq = jnp.exp(-(jnp.arange(half_width, dtype=jnp.float32) * (2.0 / vectors.shape[-1])) * math.log(500000.0))
    angles = positions.astype(jnp.float32)[:, None] * inv_freq[None, :]
    cosine = jnp.cos(angles)[:, None, :]
    sine = jnp.sin(angles)[:, None, :]
    front_half = vectors[..., :half_width]
    back_half = vectors[..., half_width:]
    return jnp.concatenate([front_half * cosine - back_half * sine, back_half * cosine + front_half * sine], -1)

def reference(tokens, norm_gain, w_query, key_matrix, value_matrix, seg_ids):
    wide_tokens = tokens.astype(jnp.float32)
    rms_normalized = (wide_tokens * lax.rsqrt(lax.optimization_barrier(jnp.mean(wide_tokens * wide_tokens, -1, keepdims=True)) + 1e-05) * norm_gain.astype(jnp.float32)).astype(jnp.bfloat16)
    positions = jnp.arange(PACKED_TOKENS, dtype=jnp.int32)
    query_raw = jnp.dot(rms_normalized, w_query, preferred_element_type=jnp.float32).reshape(PACKED_TOKENS, LOCAL_QUERY_HEADS, HEAD_SIZE)
    key_projected_raw = jnp.dot(rms_normalized, key_matrix, preferred_element_type=jnp.float32).reshape(PACKED_TOKENS, KEY_VALUE_HEADS, HEAD_SIZE)
    value_rows = jnp.dot(rms_normalized, value_matrix, preferred_element_type=jnp.float32).astype(jnp.bfloat16).reshape(PACKED_TOKENS, KEY_VALUE_HEADS, HEAD_SIZE)
    query = rotate(query_raw, positions).astype(jnp.bfloat16)
    key = rotate(key_projected_raw, positions).astype(jnp.bfloat16)
    heads_per_group = LOCAL_QUERY_HEADS // KEY_VALUE_HEADS
    row_block = math.gcd(PACKED_TOKENS, 1024)
    scale = 1.0 / math.sqrt(HEAD_SIZE)

    def one_head(head_index):
        query_head = lax.dynamic_index_in_dim(query, head_index, 1, keepdims=False)
        key_head = lax.dynamic_index_in_dim(key, head_index // heads_per_group, 1, keepdims=False)
        value_head = lax.dynamic_index_in_dim(value_rows, head_index // heads_per_group, 1, keepdims=False)

        def one_block(block_index):
            offset = block_index * row_block
            query_rows = lax.dynamic_slice_in_dim(query_head, offset, row_block, 0)
            scores = jnp.dot(query_rows, key_head.T, preferred_element_type=jnp.float32) * scale
            query_pos = offset + jnp.arange(row_block, dtype=jnp.int32)
            query_segs = lax.dynamic_slice_in_dim(seg_ids, offset, row_block, 0)
            visible = (positions[None, :] <= query_pos[:, None]) & (seg_ids[None, :] == query_segs[:, None])
            scores = jnp.where(visible, scores, -1e+30)
            peak_val = lax.optimization_barrier(jnp.max(scores, -1, keepdims=True))
            probs = jnp.where(visible, jnp.exp(scores - peak_val), 0.0)
            totals = lax.optimization_barrier(jnp.sum(probs, -1, keepdims=True))
            weighted = jnp.dot(probs.astype(jnp.bfloat16), value_head, preferred_element_type=jnp.float32)
            return (weighted / totals).astype(jnp.bfloat16)
        return lax.map(one_block, jnp.arange(PACKED_TOKENS // row_block, dtype=jnp.int32)).reshape(PACKED_TOKENS, HEAD_SIZE)
    outputs = lax.map(one_head, jnp.arange(LOCAL_QUERY_HEADS, dtype=jnp.int32))
    return jnp.transpose(outputs, (1, 0, 2)).reshape(PACKED_TOKENS, LOCAL_QUERY_HEADS * HEAD_SIZE)
```

```python
import functools
import math

import jax
import jax.numpy as jnp
import numpy as np
from jax import lax
from jax.experimental import pallas as pl
from jax.experimental.pallas import tpu as pltpu
from jax.sharding import PartitionSpec as P

HEAD = 128
MESH = pl.DeviceIdType.MESH
OFFSETS = (0, -1, 1, -2, 2, -3, 3, 4)
DOCS = 8
NEG = -(2.0**100)
LOW = -(2.0**99)
STEPS = ((0, 1), (1, 3), (3, 5), (5, 7), (7, 8))
TILE = 256


def kernel(
    sub,
    reach,
    nctx,
    nten,
    tok,
    gain,
    wq,
    wk,
    wv,
    seg,
    ctab,
    stab,
    atab,
    out,
    x,
    w,
    nrm,
    q,
    kv,
    kaug,
    lp,
    cosv,
    sinv,
    ct,
    st,
    at,
    gv,
    sv,
    acc,
    mx,
    tot,
    local_sem,
    rs_send,
    rs_recv,
    ls_send,
    ls_recv,
    own_send_sem,
    fwd_sem,
    kv_recv,
):
    f32, bf16 = jnp.float32, jnp.bfloat16
    rows = sub * nten
    half = sub // 2
    c = lax.axis_index("context")
    t = lax.axis_index("tensor")
    right = lax.rem(t + 1, nten)
    left = lax.rem(t + nten - 1, nten)
    last = nctx - 1
    wide_q = wq.shape[1]
    heads = wide_q // HEAD

    loads = [
        pltpu.make_async_copy(tok, x.at[pl.ds(0, sub)], local_sem.at[0]),
        pltpu.make_async_copy(seg, sv, local_sem.at[1]),
        pltpu.make_async_copy(gain, gv, local_sem.at[2]),
        pltpu.make_async_copy(atab, at, local_sem.at[3]),
        pltpu.make_async_copy(ctab, ct, local_sem.at[4]),
        pltpu.make_async_copy(stab, st, local_sem.at[5]),
        pltpu.make_async_copy(wq, w.at[:, pl.ds(0, wide_q)], local_sem.at[6]),
        pltpu.make_async_copy(wk, w.at[:, pl.ds(wide_q, HEAD)], local_sem.at[7]),
        pltpu.make_async_copy(wv, w.at[:, pl.ds(wide_q + HEAD, HEAD)], local_sem.at[8]),
    ]
    for one in loads:
        one.start()

    barrier = pltpu.get_barrier_semaphore()

    def greet(where):
        pl.semaphore_signal(barrier, inc=1, device_id=where, device_id_type=MESH)

    greet({"tensor": left})
    greet({"tensor": right})

    @pl.when(c >= 1)
    def _():
        greet({"context": c - 1})

    @pl.when(c < last)
    def _():
        greet({"context": c + 1})

    @pl.when(c >= reach)
    def _():
        greet({"context": c - reach})

    @pl.when(c + reach <= last)
    def _():
        greet({"context": c + reach})

    tails = [last - d for d in range(5, reach)]
    for s in tails:

        @pl.when(c == s)
        def _():
            greet({"context": last})

        @pl.when(c == last)
        def _(s=s):
            greet({"context": s})

    one = jnp.int32(1)
    zero = jnp.int32(0)
    expected = (
        2
        + jnp.where(c >= 1, one, zero)
        + jnp.where(c < last, one, zero)
        + jnp.where(c >= reach, one, zero)
        + jnp.where(c + reach <= last, one, zero)
        + jnp.where(c == last, jnp.int32(len(tails)), zero)
    )
    for s in tails:
        expected = expected + jnp.where(c == s, one, zero)
    pl.semaphore_wait(barrier, expected)

    def half_rows(slot, which):
        return pl.ds(slot * sub + which * half, half)

    def ring_copy(k, to_right):
        first = 0 if to_right else 1
        which = first if k % 2 == 0 else 1 - first
        hop = k // 2
        odd = 1 if to_right else 2
        if hop == 0:
            src = tok.at[pl.ds(which * half, half)]
        else:
            src = x.at[half_rows(2 * (hop - 1) + odd, which)]
        slot = 2 * hop + odd if hop < 3 else 7
        return pltpu.make_async_remote_copy(
            src_ref=src,
            dst_ref=x.at[half_rows(slot, which)],
            send_sem=(rs_send if to_right else ls_send).at[k],
            recv_sem=(rs_recv if to_right else ls_recv).at[k],
            device_id={"tensor": right if to_right else left},
            device_id_type=MESH,
        )

    for k in (0, 1):
        ring_copy(k, True).start()
        ring_copy(k, False).start()

    def ring_step(k):
        ring_copy(k, True).wait_recv()
        if k <= 4:
            ring_copy(k + 2, True).start()
        ring_copy(k, False).wait_recv()
        if k <= 4:
            ring_copy(k + 2, False).start()

    def part(m):
        lo, hi = STEPS[m]
        return pl.ds(lo * sub, (hi - lo) * sub)

    def kv_copy(m, src_slot, dst_slot, target, sem, recv):
        return pltpu.make_async_remote_copy(
            src_ref=kv.at[src_slot, part(m)],
            dst_ref=kv.at[dst_slot, part(m)],
            send_sem=sem,
            recv_sem=recv,
            device_id={"context": target},
            device_id_type=MESH,
        )

    def own_copies(m):
        res = [(c < last, kv_copy(m, 0, 1, c + 1, own_send_sem.at[0, m], kv_recv.at[1, m]))]
        res.append(
            (
                c + reach <= last,
                kv_copy(m, 0, reach, c + reach, own_send_sem.at[1, m], kv_recv.at[reach, m]),
            )
        )
        for d in range(5, reach):
            res.append(
                (c == last - d, kv_copy(m, 0, d, last, own_send_sem.at[1, m], kv_recv.at[d, m]))
            )
        return res

    def own_send(m):
        for cond, copy in own_copies(m):

            @pl.when(cond)
            def _(copy=copy):
                copy.start()

    def forward(m, d):
        if d <= 3:
            return (
                (c >= d) & (c < last),
                kv_copy(m, d, d + 1, c + 1, fwd_sem.at[d, m], kv_recv.at[d + 1, m]),
            )
        if d >= 6:
            return (
                c >= d,
                kv_copy(m, d, d - 1, c - 1, fwd_sem.at[d, m], kv_recv.at[d - 1, m]),
            )
        return None

    def relay(m, d):
        @pl.when(c >= d)
        def _():
            kv_copy(m, d, d, c, fwd_sem.at[d, m], kv_recv.at[d, m]).wait_recv()

        f = forward(m, d)
        if f is not None:

            @pl.when(f[0])
            def _():
                f[1].start()

    def hop(m, h):
        relay(m, h)
        relay(m, reach + 1 - h)

    lane = lax.broadcasted_iota(jnp.int32, (1, HEAD), 1)
    places = [lax.rem(t + o + nten, nten) * sub for o in OFFSETS]
    for a in range(nten):
        lp[a * sub : (a + 1) * sub, :] = (
            places[a] + lax.broadcasted_iota(jnp.int32, (sub, HEAD), 0)
        ).astype(f32)
    for i in (1, 3, 4, 5):
        loads[i].wait()
    total_rows = nctx * rows
    segv = sv[...]
    begin = jnp.where(lane >= DOCS, f32(total_rows), f32(0.0))
    end = jnp.full((1, HEAD), total_rows, f32)
    for e in range(1, DOCS):
        count = jnp.sum(jnp.where(segv < e, f32(1.0), f32(0.0)))
        begin = jnp.where(lane == e, count, begin)
        end = jnp.where(lane == e - 1, count, end)
    for d in range(reach + 1):
        base = ((c - d) * rows).astype(f32)

        @pl.when(c >= d)
        def _():
            here = lp[...] + base
            kaug[d] = jnp.where((here >= begin) & (here < end), f32(1.0), f32(0.0)).astype(bf16)

    qaug = jnp.where(kaug[0].astype(f32) > 0.5, f32(0.0), f32(NEG)).astype(bf16)
    for h in range(heads):
        q[h * rows : (h + 1) * rows, HEAD : 2 * HEAD] = qaug
    mine = lax.broadcasted_iota(jnp.int32, (nctx, 2 * HEAD), 0) == c
    both = jnp.sum(jnp.where(mine, at[...], 0.0), 0, keepdims=True)
    ca, sa = both[:, 0:HEAD], both[:, HEAD : 2 * HEAD]
    sign = jnp.where(lane < HEAD // 2, f32(-1.0), f32(1.0))
    for a in range(nten):
        here = pl.ds(pl.multiple_of(places[a], sub), sub)
        cb, sb = ct[here, :], st[here, :]
        cosv[a * sub : (a + 1) * sub, :] = ca * cb - sa * sb
        sinv[a * sub : (a + 1) * sub, :] = (sa * cb + ca * sb) * sign

    def project(m):
        lo, hi = STEPS[m]
        r0, n = lo * sub, (hi - lo) * sub

        def norm(i, carry):
            v = x[pl.ds(r0 + i * 16, 16), :].astype(f32)
            mean = jnp.sum(v * v, -1, keepdims=True) * (1.0 / v.shape[1])
            nrm[pl.ds(i * 16, 16), :] = (v * lax.rsqrt(mean + 1e-05) * gv[...].astype(f32)).astype(
                bf16
            )
            return carry

        lax.fori_loop(0, n // 16, norm, 0)
        got = jnp.dot(nrm[0:n, :], w[...], preferred_element_type=f32)
        cs, sn = cosv[r0 : r0 + n, :], sinv[r0 : r0 + n, :]

        def rotate(v):
            return (v * cs + pltpu.roll(v, HEAD // 2, 1) * sn).astype(bf16)

        for h in range(heads):
            q[h * rows + r0 : h * rows + r0 + n, 0:HEAD] = rotate(got[:, h * HEAD : (h + 1) * HEAD])
        kv[0, r0 : r0 + n, 0:HEAD] = rotate(got[:, wide_q : wide_q + HEAD])
        kv[0, r0 : r0 + n, HEAD : 2 * HEAD] = got[:, wide_q + HEAD :].astype(bf16)

    scale = math.log2(math.e) / math.sqrt(HEAD)
    acc[...] = jnp.zeros_like(acc)
    tot[...] = jnp.zeros_like(tot)
    mx[...] = jnp.full_like(mx, LOW)
    col = lax.broadcasted_iota(jnp.int32, (1, rows), 1)
    kpos = jnp.zeros((1, rows), jnp.int32)
    for a in range(nten):
        kpos = jnp.where((col >= a * sub) & (col < (a + 1) * sub), places[a] + col - a * sub, kpos)
    kpos = kpos.astype(f32)

    def attend(d):
        @pl.when(c >= d)
        def _():
            keys = jnp.concatenate([kv[d, :, 0:HEAD], kaug[d]], 1)
            vals = kv[d, :, HEAD : 2 * HEAD]
            for i in range(heads * rows // TILE):
                at_rows = slice(i * TILE, (i + 1) * TILE)
                s = (
                    lax.dot_general(
                        q[at_rows, :], keys, (((1,), (1,)), ((), ())), preferred_element_type=f32
                    )
                    * scale
                )
                if d == 0:
                    r = (i * TILE) % rows
                    s = jnp.where(kpos <= lp[r : r + TILE, 0:1], s, NEG)
                old = mx[at_rows, 0:1]
                new = jnp.maximum(old, jnp.max(s, -1, keepdims=True))
                p = jnp.exp2(s - new)
                fade = jnp.exp2(old - new)
                mx[at_rows, 0:1] = new
                tot[at_rows, 0:1] = tot[at_rows, 0:1] * fade + jnp.sum(p, -1, keepdims=True)
                acc[at_rows, :] = acc[at_rows, :] * fade + jnp.dot(
                    p.astype(bf16), vals, preferred_element_type=f32
                )

    for i in (0, 2, 6, 7, 8):
        loads[i].wait()
    project(0)
    own_send(0)
    ring_step(0)
    hop(0, 1)
    ring_step(1)
    project(1)
    own_send(1)
    hop(0, 2)
    ring_step(2)
    hop(0, 3)
    hop(1, 1)
    ring_step(3)
    project(2)
    own_send(2)
    hop(0, 4)
    hop(1, 2)
    ring_step(4)
    hop(1, 3)
    hop(2, 1)
    ring_step(5)
    project(3)
    own_send(3)
    hop(1, 4)
    hop(2, 2)
    hop(2, 3)
    hop(2, 4)
    hop(3, 1)
    hop(3, 2)
    hop(3, 3)
    ring_step(6)
    project(4)
    own_send(4)
    hop(3, 4)
    attend(0)
    for h in range(1, 5):
        hop(4, h)
        attend(h)
        attend(reach + 1 - h)

    for h in range(heads):
        for a in range(nten):
            r = h * rows + a * sub
            done = acc[r : r + sub, :] / tot[r : r + sub, 0:1]
            out[pl.ds(pl.multiple_of(places[a], sub), sub), h * HEAD : (h + 1) * HEAD] = (
                done.astype(bf16)
            )

    for k in range(7):
        ring_copy(k, True).wait_send()
        ring_copy(k, False).wait_send()
    for m in range(len(STEPS)):
        waits = own_copies(m) + [forward(m, d) for d in (1, 2, 3, 6, 7, 8)]
        for cond, copy in waits:

            @pl.when(cond)
            def _(copy=copy):
                copy.wait_send()


def tables(rows, nctx):
    freq = np.exp(-(np.arange(HEAD // 2) * (2.0 / HEAD)) * math.log(500000.0))
    fine = np.arange(rows)[:, None] * freq[None, :]
    coarse = (np.arange(nctx) * rows)[:, None] * freq[None, :]
    twice = lambda v: np.concatenate([v, v], 1).astype(np.float32)
    both = np.concatenate([twice(np.cos(coarse)), twice(np.sin(coarse))], 1)
    return twice(np.cos(fine)), twice(np.sin(fine)), both


def solution(mesh):
    nctx, nten = mesh.shape["context"], mesh.shape["tensor"]

    def body(tokens, norm_gain, w_query, key_matrix, value_matrix, seg_ids):
        sub, width = tokens.shape
        rows = sub * nten
        wide_q = w_query.shape[1]
        heads = wide_q // HEAD
        reach = 4096 // rows
        ctab, stab, atab = tables(rows, nctx)

        hbm = pl.BlockSpec(memory_space=pl.ANY)
        dma = pltpu.SemaphoreType.DMA
        f32, bf16 = jnp.float32, jnp.bfloat16
        return pl.pallas_call(
            functools.partial(kernel, sub, reach, nctx, nten),
            out_shape=jax.ShapeDtypeStruct((rows, wide_q), bf16),
            in_specs=[hbm] * 9,
            out_specs=pl.BlockSpec(memory_space=pltpu.VMEM),
            scratch_shapes=[
                pltpu.VMEM((rows, width), bf16),
                pltpu.VMEM((width, wide_q + 2 * HEAD), bf16),
                pltpu.VMEM((2 * sub, width), bf16),
                pltpu.VMEM((heads * rows, 2 * HEAD), bf16),
                pltpu.VMEM((reach + 1, rows, 2 * HEAD), bf16),
                pltpu.VMEM((reach + 1, rows, HEAD), bf16),
                pltpu.VMEM((rows, HEAD), f32),
                pltpu.VMEM((rows, HEAD), f32),
                pltpu.VMEM((rows, HEAD), f32),
                pltpu.VMEM((rows, HEAD), f32),
                pltpu.VMEM((rows, HEAD), f32),
                pltpu.VMEM((nctx, 2 * HEAD), f32),
                pltpu.VMEM((1, width), bf16),
                pltpu.VMEM((seg_ids.shape[0] // HEAD, HEAD), jnp.int32),
                pltpu.VMEM((heads * rows, HEAD), f32),
                pltpu.VMEM((heads * rows, HEAD), f32),
                pltpu.VMEM((heads * rows, HEAD), f32),
                dma((9,)),
                dma((7,)),
                dma((7,)),
                dma((7,)),
                dma((7,)),
                dma((2, len(STEPS))),
                dma((reach + 1, len(STEPS))),
                dma((reach + 1, len(STEPS))),
            ],
            compiler_params=pltpu.CompilerParams(
                collective_id=0, has_side_effects=True, vmem_limit_bytes=60 << 20
            ),
        )(
            tokens,
            norm_gain.reshape(1, width),
            w_query,
            key_matrix,
            value_matrix,
            seg_ids.reshape(-1, HEAD),
            ctab,
            stab,
            atab,
        )

    in_specs = (
        P(("dp", "context", "tensor"), None),
        P(),
        P(None, "tensor"),
        P(None, "tensor"),
        P(None, "tensor"),
        P("dp"),
    )
    out_specs = P(("dp", "context"), "tensor")
    return jax.shard_map(body, mesh=mesh, in_specs=in_specs, out_specs=out_specs, check_vma=False)
```

```python
import functools
import math

import jax
import jax.numpy as jnp
import numpy as np
from jax import lax
from jax.experimental import pallas as pl
from jax.experimental.pallas import tpu as pltpu
from jax.sharding import PartitionSpec as P

HEAD = 128
MESH = pl.DeviceIdType.MESH
DOCS = 8
NEG = -(2.0**100)
LOW = -(2.0**99)
ARRIVAL = [(0, 0), (0, 1)]
for _k in range(7):
    ARRIVAL += [(-(1 + _k // 2), _k % 2), (1 + _k // 2, 1 - _k % 2)]
DIRECT = (1, 2, 7, 8)
PASSED = {2: ((1, 3), (2, 4)), 7: ((-1, 6), (-2, 5))}
EXTRA = ((6, 6), (6, 5), (5, 5))
WAITED = (1, 3, 4, 5, 6, 8)
RING = PROJ = KV = ATT = True


def kernel(
    sub,
    reach,
    nctx,
    nten,
    tok,
    gain,
    wq,
    wk,
    wv,
    seg,
    ctab,
    stab,
    atab,
    out,
    x,
    w,
    nrm,
    q,
    kv,
    kaug,
    lp,
    qp,
    kp,
    cosv,
    sinv,
    ct,
    st,
    at,
    gv,
    sv,
    acc,
    mx,
    tot,
    local_sem,
    rs_send,
    rs_recv,
    ls_send,
    ls_recv,
    own_sem,
    fwd_sem,
    kv_recv,
):
    f32, bf16 = jnp.float32, jnp.bfloat16
    rows = sub * nten
    half = sub // 2
    c = lax.axis_index("context")
    t = lax.axis_index("tensor")
    right = lax.rem(t + 1, nten)
    left = lax.rem(t + nten - 1, nten)
    last = nctx - 1
    wide_q = wq.shape[1]
    heads = wide_q // HEAD
    msgs = nten
    slots = reach + 1
    tile = heads * sub

    loads = [
        pltpu.make_async_copy(tok, x.at[pl.ds(0, sub)], local_sem.at[0]),
        pltpu.make_async_copy(seg, sv, local_sem.at[1]),
        pltpu.make_async_copy(gain, gv, local_sem.at[2]),
        pltpu.make_async_copy(atab, at, local_sem.at[3]),
        pltpu.make_async_copy(ctab, ct, local_sem.at[4]),
        pltpu.make_async_copy(stab, st, local_sem.at[5]),
        pltpu.make_async_copy(wq, w.at[:, pl.ds(0, wide_q)], local_sem.at[6]),
        pltpu.make_async_copy(wk, w.at[:, pl.ds(wide_q, HEAD)], local_sem.at[7]),
        pltpu.make_async_copy(wv, w.at[:, pl.ds(wide_q + HEAD, HEAD)], local_sem.at[8]),
    ]

    barrier = pltpu.get_barrier_semaphore()
    one, zero = jnp.int32(1), jnp.int32(0)
    links = [(c >= d, c - d) for d in DIRECT] + [(c + d <= last, c + d) for d in DIRECT]
    for back, d in EXTRA:
        links.append((c == last - back, c + d))
        links.append((c == last - back + d, c - d))
    for where in (left, right):
        pl.semaphore_signal(barrier, inc=1, device_id={"tensor": where}, device_id_type=MESH)
    expected = jnp.int32(2)
    for cond, where in links:

        @pl.when(cond)
        def _(where=where):
            pl.semaphore_signal(barrier, inc=1, device_id={"context": where}, device_id_type=MESH)

        expected = expected + jnp.where(cond, one, zero)
    for load in loads:
        load.start()
    pl.semaphore_wait(barrier, expected)

    def unit(u):
        return x.at[pl.ds(u * half, half)]

    def ring_copy(k, to_right):
        first = 2 if to_right else 3
        if k < 2:
            src = tok.at[pl.ds((k if to_right else 1 - k) * half, half)]
        else:
            src = unit(first + 2 * (k - 2))
        return pltpu.make_async_remote_copy(
            src_ref=src,
            dst_ref=unit(first + 2 * k),
            send_sem=(rs_send if to_right else ls_send).at[k],
            recv_sem=(rs_recv if to_right else ls_recv).at[k],
            device_id={"tensor": right if to_right else left},
            device_id_type=MESH,
        )

    def ring_step(k):
        for to_right in (True, False):
            ring_copy(k, to_right).wait_recv()
            if k <= 4:
                ring_copy(k + 2, to_right).start()

    def kv_copy(m, src_slot, dst_slot, target, sem):
        return pltpu.make_async_remote_copy(
            src_ref=kv.at[m, pl.ds(src_slot * sub, sub)],
            dst_ref=kv.at[m, pl.ds(dst_slot * sub, sub)],
            send_sem=sem,
            recv_sem=kv_recv.at[dst_slot, m],
            device_id={"context": target},
            device_id_type=MESH,
        )

    def own_copies(m):
        res = [
            (c + d <= last, kv_copy(m, 0, d, c + d, own_sem.at[i, m])) for i, d in enumerate(DIRECT)
        ]
        for back, d in EXTRA:
            res.append((c == last - back, kv_copy(m, 0, d, c + d, own_sem.at[d - 3, m])))
        return res

    def passed_copies(m, slot):
        first = 0 if slot == 2 else 2
        return [
            (
                (c >= slot) & (c + step <= last),
                kv_copy(m, slot, there, c + step, fwd_sem.at[first + i, m]),
            )
            for i, (step, there) in enumerate(PASSED[slot])
        ]

    def start_all(copies):
        for cond, copy in copies:

            @pl.when(cond)
            def _(copy=copy):
                copy.start()

    def landed(m, d):
        @pl.when(c >= d)
        def _():
            kv_copy(m, d, d, c, own_sem.at[0, m]).wait_recv()

    def own_send(m):
        start_all(own_copies(m))

    def relay(m):
        for slot in PASSED:
            landed(m, slot)
            start_all(passed_copies(m, slot))

    def arrived(m):
        for d in WAITED:
            landed(m, d)

    if RING:
        for k in (0, 1):
            ring_copy(k, True).start()
            ring_copy(k, False).start()

    lane = lax.broadcasted_iota(jnp.int32, (1, HEAD), 1)
    places = [lax.rem(t + o + nten, nten) * sub + h * half for o, h in ARRIVAL]
    for u in range(2 * nten):
        spot = (places[u] + lax.broadcasted_iota(jnp.int32, (half, HEAD), 0)).astype(f32)
        lp[u * half : (u + 1) * half, :] = spot
        for h in range(heads):
            r = (u // 2) * tile + h * sub + (u % 2) * half
            qp[r : r + half, :] = spot
    for i in (1, 3, 4, 5):
        loads[i].wait()
    total_rows = nctx * rows
    segv = sv[...]
    begin = jnp.where(lane >= DOCS, f32(total_rows), f32(0.0))
    end = jnp.full((1, HEAD), total_rows, f32)
    for e in range(1, DOCS):
        count = jnp.sum(jnp.where(segv < e, f32(1.0), f32(0.0)))
        begin = jnp.where(lane == e, count, begin)
        end = jnp.where(lane == e - 1, count, end)
    begin = jnp.where(lane == DOCS, f32(-total_rows), begin)
    end = jnp.where(lane == DOCS, f32(0.0), end)
    missing = jnp.where(lane == DOCS, f32(1.0), f32(0.0)).astype(bf16)
    mine = lax.broadcasted_iota(jnp.int32, (nctx, 2 * HEAD), 0) == c
    both = jnp.sum(jnp.where(mine, at[...], 0.0), 0, keepdims=True)
    ca, sa = both[:, 0:HEAD], both[:, HEAD : 2 * HEAD]
    sign = jnp.where(lane < HEAD // 2, f32(-1.0), f32(1.0))
    for u in range(2 * nten):
        here = pl.ds(pl.multiple_of(places[u], half), half)
        cb, sb = ct[here, :], st[here, :]
        cosv[u * half : (u + 1) * half, :] = ca * cb - sa * sb
        sinv[u * half : (u + 1) * half, :] = (sa * cb + ca * sb) * sign

    def masks(m, carry):
        local = lp[pl.ds(pl.multiple_of(m * sub, sub), sub), :]
        for d in range(slots):
            here = local + ((c - d) * rows).astype(f32)
            kaug[m, d * sub : (d + 1) * sub, :] = jnp.where(
                (here >= begin) & (here < end), f32(1.0), f32(0.0)
            ).astype(bf16)
        kaug[m, slots * sub :, :] = jnp.broadcast_to(missing, (kaug.shape[1] - slots * sub, HEAD))
        kv[m, slots * sub :, :] = jnp.zeros((kv.shape[1] - slots * sub, 2 * HEAD), bf16)
        qaug = jnp.where(kaug[m, 0:sub, :].astype(f32) > 0.5, f32(0.0), f32(NEG)).astype(bf16)
        for h in range(heads):
            r = pl.multiple_of(m * tile + h * sub, sub)
            q[pl.ds(r, sub), HEAD : 2 * HEAD] = qaug
        for d in range(1, slots):

            @pl.when(c < d)
            def _():
                kv[m, d * sub : (d + 1) * sub, :] = jnp.zeros((sub, 2 * HEAD), bf16)

        return carry

    lax.fori_loop(0, msgs, masks, 0)
    for m in range(msgs):
        spot = jnp.where(
            lane < half,
            places[2 * m] + lane,
            jnp.where(lane < sub, places[2 * m + 1] + lane - half, -1),
        ).astype(f32)
        kp[m] = jnp.broadcast_to(spot, (8, HEAD))
    acc[...] = jnp.zeros_like(acc)
    tot[...] = jnp.zeros_like(tot)
    mx[...] = jnp.full_like(mx, LOW)

    scale = math.log2(math.e) / math.sqrt(HEAD)

    def project(m):
        r0 = m * sub

        def norm(i, carry):
            v = x[pl.ds(r0 + i * 16, 16), :].astype(f32)
            mean = jnp.sum(v * v, -1, keepdims=True) * (1.0 / v.shape[1])
            nrm[pl.ds(i * 16, 16), :] = (v * lax.rsqrt(mean + 1e-05) * gv[...].astype(f32)).astype(
                bf16
            )
            return carry

        lax.fori_loop(0, sub // 16, norm, 0)
        got = jnp.dot(nrm[...], w[...], preferred_element_type=f32)
        cs, sn = cosv[r0 : r0 + sub, :], sinv[r0 : r0 + sub, :]

        def rotate(v):
            return v * cs + pltpu.roll(v, HEAD // 2, 1) * sn

        kv[m, 0:sub, 0:HEAD] = rotate(got[:, wide_q : wide_q + HEAD]).astype(bf16)
        kv[m, 0:sub, HEAD : 2 * HEAD] = got[:, wide_q + HEAD :].astype(bf16)
        for h in range(heads):
            r = m * tile + h * sub
            q[r : r + sub, 0:HEAD] = (rotate(got[:, h * HEAD : (h + 1) * HEAD]) * scale).astype(bf16)

    chunks = kv.shape[1] // HEAD

    def attend_rows(here, j):
        keys = jnp.concatenate([kv[j, :, 0:HEAD], kaug[j]], 1)
        vals = kv[j, :, HEAD : 2 * HEAD]
        s = lax.dot_general(
            q[here, :], keys, (((1,), (1,)), ((), ())), preferred_element_type=f32
        )
        cols = [s[:, i * HEAD : (i + 1) * HEAD] for i in range(chunks)]
        cols[0] = jnp.where(kp[j][0:1, :] <= qp[here, :], cols[0], NEG)
        old = mx[here, :]
        top = functools.reduce(jnp.maximum, cols)
        new = jnp.maximum(old, jnp.max(top, -1, keepdims=True))
        p = [jnp.exp2(v - new) for v in cols]
        fade = jnp.exp2(old - new)
        mx[here, :] = new
        tot[here, :] = tot[here, :] * fade + functools.reduce(jnp.add, p)
        low = jnp.concatenate([v.astype(bf16) for v in p], 1)
        acc[here, :] = acc[here, :] * fade + jnp.dot(low, vals, preferred_element_type=f32)

    def attend(lo, hi, j):
        pairs = (hi - lo) // 2

        def two(i, carry):
            r = pl.multiple_of(lo * tile + i * 2 * tile, tile)
            attend_rows(pl.ds(r, 2 * tile), j)
            return carry

        if pairs:
            lax.fori_loop(0, pairs, two, 0)
        if (hi - lo) % 2:
            attend_rows(pl.ds((hi - 1) * tile, tile), j)

    def attend_keys(i, lo, hi):
        def step(j, carry):
            attend_rows(pl.ds(i * tile, tile), j)
            return carry

        if hi > lo:
            lax.fori_loop(lo, hi, step, 0)

    for i in (0, 2, 6, 7, 8):
        loads[i].wait()
    for s in range(msgs):
        if RING and s >= 1:
            ring_step(s - 1)
        if PROJ:
            project(s)
        if KV:
            own_send(s)
            if s >= 1:
                relay(s - 1)
            if s >= 2:
                arrived(s - 2)
        if ATT and s >= 2:
            attend(0, s + 1, s - 2)
            attend_keys(s, 0, s - 2)
    for m in (msgs - 2, msgs - 1):
        if KV and m == msgs - 2:
            relay(msgs - 1)
        if KV:
            arrived(m)
        if ATT:
            attend(0, msgs, m)

    for i in range(msgs):
        for h in range(heads):
            r = i * tile + h * sub
            whole = jnp.sum(tot[r : r + sub, :], -1, keepdims=True)
            done = (acc[r : r + sub, :] / whole).astype(bf16)
            for u in (0, 1):
                there = pl.ds(pl.multiple_of(places[2 * i + u], half), half)
                out[there, h * HEAD : (h + 1) * HEAD] = done[u * half : (u + 1) * half]

    if RING:
        for k in range(7):
            ring_copy(k, True).wait_send()
            ring_copy(k, False).wait_send()
    if KV:
        for m in range(msgs):
            for cond, copy in own_copies(m) + passed_copies(m, 2) + passed_copies(m, 7):

                @pl.when(cond)
                def _(copy=copy):
                    copy.wait_send()


def tables(rows, nctx):
    freq = np.exp(-(np.arange(HEAD // 2) * (2.0 / HEAD)) * math.log(500000.0))
    fine = np.arange(rows)[:, None] * freq[None, :]
    coarse = (np.arange(nctx) * rows)[:, None] * freq[None, :]
    twice = lambda v: np.concatenate([v, v], 1).astype(np.float32)
    both = np.concatenate([twice(np.cos(coarse)), twice(np.sin(coarse))], 1)
    return twice(np.cos(fine)), twice(np.sin(fine)), both


def solution(mesh):
    nctx, nten = mesh.shape["context"], mesh.shape["tensor"]

    def body(tokens, norm_gain, w_query, key_matrix, value_matrix, seg_ids):
        sub, width = tokens.shape
        rows = sub * nten
        wide_q = w_query.shape[1]
        heads = wide_q // HEAD
        reach = 4096 // rows
        key_rows = pl.cdiv((reach + 1) * sub, HEAD) * HEAD
        ctab, stab, atab = tables(rows, nctx)

        hbm = pl.BlockSpec(memory_space=pl.ANY)
        dma = pltpu.SemaphoreType.DMA
        f32, bf16 = jnp.float32, jnp.bfloat16
        return pl.pallas_call(
            functools.partial(kernel, sub, reach, nctx, nten),
            out_shape=jax.ShapeDtypeStruct((rows, wide_q), bf16),
            in_specs=[hbm] * 9,
            out_specs=pl.BlockSpec(memory_space=pltpu.VMEM),
            scratch_shapes=[
                pltpu.VMEM((rows, width), bf16),
                pltpu.VMEM((width, wide_q + 2 * HEAD), bf16),
                pltpu.VMEM((sub, width), bf16),
                pltpu.VMEM((heads * rows, 2 * HEAD), bf16),
                pltpu.VMEM((nten, key_rows, 2 * HEAD), bf16),
                pltpu.VMEM((nten, key_rows, HEAD), bf16),
                pltpu.VMEM((rows, HEAD), f32),
                pltpu.VMEM((heads * rows, HEAD), f32),
                pltpu.VMEM((nten, 8, HEAD), f32),
                pltpu.VMEM((rows, HEAD), f32),
                pltpu.VMEM((rows, HEAD), f32),
                pltpu.VMEM((rows, HEAD), f32),
                pltpu.VMEM((rows, HEAD), f32),
                pltpu.VMEM((nctx, 2 * HEAD), f32),
                pltpu.VMEM((1, width), bf16),
                pltpu.VMEM((seg_ids.shape[0] // HEAD, HEAD), jnp.int32),
                pltpu.VMEM((heads * rows, HEAD), f32),
                pltpu.VMEM((heads * rows, HEAD), f32),
                pltpu.VMEM((heads * rows, HEAD), f32),
                dma((9,)),
                dma((7,)),
                dma((7,)),
                dma((7,)),
                dma((7,)),
                dma((4, nten)),
                dma((4, nten)),
                dma((reach + 1, nten)),
            ],
            compiler_params=pltpu.CompilerParams(
                collective_id=0, has_side_effects=True, vmem_limit_bytes=60 << 20
            ),
        )(
            tokens,
            norm_gain.reshape(1, width),
            w_query,
            key_matrix,
            value_matrix,
            seg_ids.reshape(-1, HEAD),
            ctab,
            stab,
            atab,
        )

    in_specs = (
        P(("dp", "context", "tensor"), None),
        P(),
        P(None, "tensor"),
        P(None, "tensor"),
        P(None, "tensor"),
        P("dp"),
    )
    out_specs = P(("dp", "context"), "tensor")
    return jax.shard_map(body, mesh=mesh, in_specs=in_specs, out_specs=out_specs, check_vma=False)
```

```python
import functools
import math

import jax
import jax.numpy as jnp
import numpy as np
from jax import lax
from jax.experimental import pallas as pl
from jax.experimental.pallas import tpu as pltpu
from jax.sharding import PartitionSpec as P

HEAD = 128
MESH = pl.DeviceIdType.MESH
DOCS = 8
NEG = -(2.0**100)
LOW = -(2.0**99)
ARRIVAL = [(0, 0), (0, 1)]
for _k in range(7):
    ARRIVAL += [(-(1 + _k // 2), _k % 2), (1 + _k // 2, 1 - _k % 2)]
DIRECT = (1, 2, 7, 8)
PASSED = {2: ((1, 3), (2, 4)), 7: ((-1, 6), (-2, 5))}
EXTRA = ((6, 6), (6, 5), (5, 5))
WAITED = (1, 3, 4, 5, 6, 8)
PLAN = {
    4: ((0, 4, 0, 1, 2),),
    5: ((0, 4, 3),),
    6: ((0, 4, 4), (4, 6, 0, 1, 2, 3, 4)),
    7: ((6, 8, 0, 1, 2, 3, 4), (0, 4, 5), (4, 8, 5)),
    8: ((0, 4, 6), (4, 8, 6)),
    9: ((0, 4, 7), (4, 8, 7)),
}
RING = PROJ = KV = ATT = True


def kernel(
    sub,
    reach,
    nctx,
    nten,
    tok,
    gain,
    wq,
    wk,
    wv,
    seg,
    ctab,
    stab,
    atab,
    out,
    x,
    w,
    nrm,
    q,
    kv,
    kaug,
    lp,
    qp,
    kp,
    cosv,
    sinv,
    ct,
    st,
    at,
    gv,
    sv,
    acc,
    mx,
    tot,
    local_sem,
    rs_send,
    rs_recv,
    ls_send,
    ls_recv,
    own_sem,
    fwd_sem,
    kv_recv,
):
    f32, bf16 = jnp.float32, jnp.bfloat16
    rows = sub * nten
    half = sub // 2
    c = lax.axis_index("context")
    t = lax.axis_index("tensor")
    right = lax.rem(t + 1, nten)
    left = lax.rem(t + nten - 1, nten)
    last = nctx - 1
    wide_q = wq.shape[1]
    heads = wide_q // HEAD
    msgs = nten
    slots = reach + 1
    tile = heads * sub

    loads = [
        pltpu.make_async_copy(tok, x.at[pl.ds(0, sub)], local_sem.at[0]),
        pltpu.make_async_copy(seg, sv, local_sem.at[1]),
        pltpu.make_async_copy(gain, gv, local_sem.at[2]),
        pltpu.make_async_copy(atab, at, local_sem.at[3]),
        pltpu.make_async_copy(ctab, ct, local_sem.at[4]),
        pltpu.make_async_copy(stab, st, local_sem.at[5]),
        pltpu.make_async_copy(wq, w.at[:, pl.ds(0, wide_q)], local_sem.at[6]),
        pltpu.make_async_copy(wk, w.at[:, pl.ds(wide_q, HEAD)], local_sem.at[7]),
        pltpu.make_async_copy(wv, w.at[:, pl.ds(wide_q + HEAD, HEAD)], local_sem.at[8]),
    ]

    barrier = pltpu.get_barrier_semaphore()
    one, zero = jnp.int32(1), jnp.int32(0)
    links = [(c >= d, c - d) for d in DIRECT] + [(c + d <= last, c + d) for d in DIRECT]
    for back, d in EXTRA:
        links.append((c == last - back, c + d))
        links.append((c == last - back + d, c - d))
    for where in (left, right):
        pl.semaphore_signal(barrier, inc=1, device_id={"tensor": where}, device_id_type=MESH)
    expected = jnp.int32(2)
    for cond, where in links:

        @pl.when(cond)
        def _(where=where):
            pl.semaphore_signal(barrier, inc=1, device_id={"context": where}, device_id_type=MESH)

        expected = expected + jnp.where(cond, one, zero)
    for load in loads:
        load.start()
    pl.semaphore_wait(barrier, expected)

    def unit(u):
        return x.at[pl.ds(u * half, half)]

    def ring_copy(k, to_right):
        first = 2 if to_right else 3
        if k < 2:
            src = tok.at[pl.ds((k if to_right else 1 - k) * half, half)]
        else:
            src = unit(first + 2 * (k - 2))
        return pltpu.make_async_remote_copy(
            src_ref=src,
            dst_ref=unit(first + 2 * k),
            send_sem=(rs_send if to_right else ls_send).at[k],
            recv_sem=(rs_recv if to_right else ls_recv).at[k],
            device_id={"tensor": right if to_right else left},
            device_id_type=MESH,
        )

    def ring_step(k):
        for to_right in (True, False):
            ring_copy(k, to_right).wait_recv()
            if k <= 4:
                ring_copy(k + 2, to_right).start()

    def kv_copy(m, src_slot, dst_slot, target, sem):
        return pltpu.make_async_remote_copy(
            src_ref=kv.at[m, pl.ds(src_slot * sub, sub)],
            dst_ref=kv.at[m, pl.ds(dst_slot * sub, sub)],
            send_sem=sem,
            recv_sem=kv_recv.at[dst_slot, m],
            device_id={"context": target},
            device_id_type=MESH,
        )

    def own_copies(m):
        res = [
            (c + d <= last, kv_copy(m, 0, d, c + d, own_sem.at[i, m])) for i, d in enumerate(DIRECT)
        ]
        for back, d in EXTRA:
            res.append((c == last - back, kv_copy(m, 0, d, c + d, own_sem.at[d - 3, m])))
        return res

    def passed_copies(m, slot):
        first = 0 if slot == 2 else 2
        return [
            (
                (c >= slot) & (c + step <= last),
                kv_copy(m, slot, there, c + step, fwd_sem.at[first + i, m]),
            )
            for i, (step, there) in enumerate(PASSED[slot])
        ]

    def start_all(copies):
        for cond, copy in copies:

            @pl.when(cond)
            def _(copy=copy):
                copy.start()

    def landed(m, d):
        @pl.when(c >= d)
        def _():
            kv_copy(m, d, d, c, own_sem.at[0, m]).wait_recv()

    def own_send(m):
        start_all(own_copies(m))

    def relay(m):
        for slot in PASSED:
            landed(m, slot)
            start_all(passed_copies(m, slot))

    def arrived(m):
        for d in WAITED:
            landed(m, d)

    if RING:
        for k in (0, 1):
            ring_copy(k, True).start()
            ring_copy(k, False).start()

    lane = lax.broadcasted_iota(jnp.int32, (1, HEAD), 1)
    places = [lax.rem(t + o + nten, nten) * sub + h * half for o, h in ARRIVAL]
    for u in range(2 * nten):
        spot = (places[u] + lax.broadcasted_iota(jnp.int32, (half, HEAD), 0)).astype(f32)
        lp[u * half : (u + 1) * half, :] = spot
        for h in range(heads):
            r = (u // 2) * tile + h * sub + (u % 2) * half
            qp[r : r + half, :] = spot
    for i in (1, 3, 4, 5):
        loads[i].wait()
    total_rows = nctx * rows
    segv = sv[...]
    begin = jnp.where(lane >= DOCS, f32(total_rows), f32(0.0))
    end = jnp.full((1, HEAD), total_rows, f32)
    for e in range(1, DOCS):
        count = jnp.sum(jnp.where(segv < e, f32(1.0), f32(0.0)))
        begin = jnp.where(lane == e, count, begin)
        end = jnp.where(lane == e - 1, count, end)
    begin = jnp.where(lane == DOCS, f32(-total_rows), begin)
    end = jnp.where(lane == DOCS, f32(0.0), end)
    missing = jnp.where(lane == DOCS, f32(1.0), f32(0.0)).astype(bf16)
    mine = lax.broadcasted_iota(jnp.int32, (nctx, 2 * HEAD), 0) == c
    both = jnp.sum(jnp.where(mine, at[...], 0.0), 0, keepdims=True)
    ca, sa = both[:, 0:HEAD], both[:, HEAD : 2 * HEAD]
    sign = jnp.where(lane < HEAD // 2, f32(-1.0), f32(1.0))
    for u in range(2 * nten):
        here = pl.ds(pl.multiple_of(places[u], half), half)
        cb, sb = ct[here, :], st[here, :]
        cosv[u * half : (u + 1) * half, :] = ca * cb - sa * sb
        sinv[u * half : (u + 1) * half, :] = (sa * cb + ca * sb) * sign

    def masks(m, carry):
        local = lp[pl.ds(pl.multiple_of(m * sub, sub), sub), :]
        for d in range(slots):
            here = local + ((c - d) * rows).astype(f32)
            kaug[m, d * sub : (d + 1) * sub, :] = jnp.where(
                (here >= begin) & (here < end), f32(1.0), f32(0.0)
            ).astype(bf16)
        kaug[m, slots * sub :, :] = jnp.broadcast_to(missing, (kaug.shape[1] - slots * sub, HEAD))
        kv[m, slots * sub :, :] = jnp.zeros((kv.shape[1] - slots * sub, 2 * HEAD), bf16)
        qaug = jnp.where(kaug[m, 0:sub, :].astype(f32) > 0.5, f32(0.0), f32(NEG)).astype(bf16)
        for h in range(heads):
            r = pl.multiple_of(m * tile + h * sub, sub)
            q[pl.ds(r, sub), HEAD : 2 * HEAD] = qaug
        for d in range(1, slots):

            @pl.when(c < d)
            def _():
                kv[m, d * sub : (d + 1) * sub, :] = jnp.zeros((sub, 2 * HEAD), bf16)

        return carry

    lax.fori_loop(0, msgs, masks, 0)
    for m in range(msgs):
        spot = jnp.where(
            lane < half,
            places[2 * m] + lane,
            jnp.where(lane < sub, places[2 * m + 1] + lane - half, -1),
        ).astype(f32)
        kp[m] = jnp.broadcast_to(spot, (8, HEAD))
    acc[...] = jnp.zeros_like(acc)
    tot[...] = jnp.zeros_like(tot)
    mx[...] = jnp.full_like(mx, LOW)

    scale = math.log2(math.e) / math.sqrt(HEAD)

    def project(m):
        r0 = m * sub

        def norm(i, carry):
            v = x[pl.ds(r0 + i * 16, 16), :].astype(f32)
            mean = jnp.sum(v * v, -1, keepdims=True) * (1.0 / v.shape[1])
            nrm[pl.ds(i * 16, 16), :] = (v * lax.rsqrt(mean + 1e-05) * gv[...].astype(f32)).astype(
                bf16
            )
            return carry

        lax.fori_loop(0, sub // 16, norm, 0)
        got = jnp.dot(nrm[...], w[...], preferred_element_type=f32)
        cs, sn = cosv[r0 : r0 + sub, :], sinv[r0 : r0 + sub, :]

        def rotate(v):
            return v * cs + pltpu.roll(v, HEAD // 2, 1) * sn

        kv[m, 0:sub, 0:HEAD] = rotate(got[:, wide_q : wide_q + HEAD]).astype(bf16)
        kv[m, 0:sub, HEAD : 2 * HEAD] = got[:, wide_q + HEAD :].astype(bf16)
        for h in range(heads):
            r = m * tile + h * sub
            q[r : r + sub, 0:HEAD] = (rotate(got[:, h * HEAD : (h + 1) * HEAD]) * scale).astype(bf16)

    chunks = kv.shape[1] // HEAD

    def attend(lo, hi, *js):
        here = slice(lo * tile, hi * tile)
        queries, spots = q[here, :], qp[here, :]
        cols = []
        for j in js:
            keys = jnp.concatenate([kv[j, :, 0:HEAD], kaug[j]], 1)
            s = lax.dot_general(queries, keys, (((1,), (1,)), ((), ())), preferred_element_type=f32)
            new = [s[:, i * HEAD : (i + 1) * HEAD] for i in range(chunks)]
            new[0] = jnp.where(kp[j][0:1, :] <= spots, new[0], NEG)
            cols.append(new)
        old = mx[here, :]
        top = functools.reduce(jnp.maximum, sum(cols, []))
        new = jnp.maximum(old, jnp.max(top, -1, keepdims=True))
        fade = jnp.exp2(old - new)
        mx[here, :] = new
        whole, got = tot[here, :] * fade, acc[here, :] * fade
        for j, part in zip(js, cols):
            p = [jnp.exp2(v - new) for v in part]
            whole = whole + functools.reduce(jnp.add, p)
            low = jnp.concatenate([v.astype(bf16) for v in p], 1)
            got = got + jnp.dot(low, kv[j, :, HEAD : 2 * HEAD], preferred_element_type=f32)
        tot[here, :] = whole
        acc[here, :] = got

    for i in (0, 2, 6, 7, 8):
        loads[i].wait()
    for s in range(msgs):
        if RING and s >= 1:
            ring_step(s - 1)
        if PROJ:
            project(s)
        if KV:
            own_send(s)
            if s >= 1:
                relay(s - 1)
            if s >= 2:
                arrived(s - 2)
        if ATT:
            for job in PLAN.get(s, ()):
                attend(*job)
    for m in (msgs - 2, msgs - 1):
        if KV and m == msgs - 2:
            relay(msgs - 1)
        if KV:
            arrived(m)
        if ATT:
            for job in PLAN[m + 2]:
                attend(*job)

    for i in range(msgs):
        for h in range(heads):
            r = i * tile + h * sub
            whole = jnp.sum(tot[r : r + sub, :], -1, keepdims=True)
            done = (acc[r : r + sub, :] / whole).astype(bf16)
            for u in (0, 1):
                there = pl.ds(pl.multiple_of(places[2 * i + u], half), half)
                out[there, h * HEAD : (h + 1) * HEAD] = done[u * half : (u + 1) * half]

    if RING:
        for k in range(7):
            ring_copy(k, True).wait_send()
            ring_copy(k, False).wait_send()
    if KV:
        for m in range(msgs):
            for cond, copy in own_copies(m) + passed_copies(m, 2) + passed_copies(m, 7):

                @pl.when(cond)
                def _(copy=copy):
                    copy.wait_send()


def tables(rows, nctx):
    freq = np.exp(-(np.arange(HEAD // 2) * (2.0 / HEAD)) * math.log(500000.0))
    fine = np.arange(rows)[:, None] * freq[None, :]
    coarse = (np.arange(nctx) * rows)[:, None] * freq[None, :]
    twice = lambda v: np.concatenate([v, v], 1).astype(np.float32)
    both = np.concatenate([twice(np.cos(coarse)), twice(np.sin(coarse))], 1)
    return twice(np.cos(fine)), twice(np.sin(fine)), both


def solution(mesh):
    nctx, nten = mesh.shape["context"], mesh.shape["tensor"]

    def body(tokens, norm_gain, w_query, key_matrix, value_matrix, seg_ids):
        sub, width = tokens.shape
        rows = sub * nten
        wide_q = w_query.shape[1]
        heads = wide_q // HEAD
        reach = 4096 // rows
        key_rows = pl.cdiv((reach + 1) * sub, HEAD) * HEAD
        ctab, stab, atab = tables(rows, nctx)

        hbm = pl.BlockSpec(memory_space=pl.ANY)
        dma = pltpu.SemaphoreType.DMA
        f32, bf16 = jnp.float32, jnp.bfloat16
        return pl.pallas_call(
            functools.partial(kernel, sub, reach, nctx, nten),
            out_shape=jax.ShapeDtypeStruct((rows, wide_q), bf16),
            in_specs=[hbm] * 9,
            out_specs=pl.BlockSpec(memory_space=pltpu.VMEM),
            scratch_shapes=[
                pltpu.VMEM((rows, width), bf16),
                pltpu.VMEM((width, wide_q + 2 * HEAD), bf16),
                pltpu.VMEM((sub, width), bf16),
                pltpu.VMEM((heads * rows, 2 * HEAD), bf16),
                pltpu.VMEM((nten, key_rows, 2 * HEAD), bf16),
                pltpu.VMEM((nten, key_rows, HEAD), bf16),
                pltpu.VMEM((rows, HEAD), f32),
                pltpu.VMEM((heads * rows, HEAD), f32),
                pltpu.VMEM((nten, 8, HEAD), f32),
                pltpu.VMEM((rows, HEAD), f32),
                pltpu.VMEM((rows, HEAD), f32),
                pltpu.VMEM((rows, HEAD), f32),
                pltpu.VMEM((rows, HEAD), f32),
                pltpu.VMEM((nctx, 2 * HEAD), f32),
                pltpu.VMEM((1, width), bf16),
                pltpu.VMEM((seg_ids.shape[0] // HEAD, HEAD), jnp.int32),
                pltpu.VMEM((heads * rows, HEAD), f32),
                pltpu.VMEM((heads * rows, HEAD), f32),
                pltpu.VMEM((heads * rows, HEAD), f32),
                dma((9,)),
                dma((7,)),
                dma((7,)),
                dma((7,)),
                dma((7,)),
                dma((4, nten)),
                dma((4, nten)),
                dma((reach + 1, nten)),
            ],
            compiler_params=pltpu.CompilerParams(
                collective_id=0, has_side_effects=True, vmem_limit_bytes=60 << 20
            ),
        )(
            tokens,
            norm_gain.reshape(1, width),
            w_query,
            key_matrix,
            value_matrix,
            seg_ids.reshape(-1, HEAD),
            ctab,
            stab,
            atab,
        )

    in_specs = (
        P(("dp", "context", "tensor"), None),
        P(),
        P(None, "tensor"),
        P(None, "tensor"),
        P(None, "tensor"),
        P("dp"),
    )
    out_specs = P(("dp", "context"), "tensor")
    return jax.shard_map(body, mesh=mesh, in_specs=in_specs, out_specs=out_specs, check_vma=False)
```

```python
import functools
import math

import jax
import jax.numpy as jnp
import numpy as np
from jax import lax
from jax.experimental import pallas as pl
from jax.experimental.pallas import tpu as pltpu
from jax.sharding import PartitionSpec as P

HEAD = 128
MESH = pl.DeviceIdType.MESH
DOCS = 8
NEG = -(2.0**100)
LOW = -(2.0**99)
ARRIVAL = [(0, 0), (0, 1)]
for _k in range(7):
    ARRIVAL += [(-(1 + _k // 2), _k % 2), (1 + _k // 2, 1 - _k % 2)]
DIRECT = (2, 7, 1, 8)
PASSED = {2: ((1, 3), (2, 4)), 7: ((-1, 6), (-2, 5))}
EXTRA = ((6, 6), (6, 5), (5, 5))
WAITED = (1, 3, 4, 5, 6, 8)
PLAN = {
    4: ((0, 4, 0, 1, 2),),
    5: ((0, 4, 3),),
    6: ((0, 4, 4), (4, 6, 0, 1, 2, 3, 4)),
    7: ((6, 8, 0, 1, 2, 3, 4), (0, 4, 5), (4, 8, 5)),
    8: ((0, 4, 6), (4, 8, 6)),
    9: ((0, 4, 7), (4, 8, 7)),
}
RING = PROJ = KV = ATT = True


def kernel(
    sub,
    reach,
    nctx,
    nten,
    tok,
    gain,
    wq,
    wk,
    wv,
    seg,
    ctab,
    stab,
    atab,
    out,
    x,
    w,
    nrm,
    q,
    kv,
    kaug,
    lp,
    qp,
    kp,
    cosv,
    sinv,
    ct,
    st,
    at,
    gv,
    sv,
    acc,
    mx,
    tot,
    local_sem,
    rs_send,
    rs_recv,
    ls_send,
    ls_recv,
    own_sem,
    fwd_sem,
    kv_recv,
):
    f32, bf16 = jnp.float32, jnp.bfloat16
    rows = sub * nten
    half = sub // 2
    c = lax.axis_index("context")
    t = lax.axis_index("tensor")
    right = lax.rem(t + 1, nten)
    left = lax.rem(t + nten - 1, nten)
    last = nctx - 1
    wide_q = wq.shape[1]
    heads = wide_q // HEAD
    msgs = nten
    slots = reach + 1
    tile = heads * sub

    loads = [
        pltpu.make_async_copy(tok, x.at[pl.ds(0, sub)], local_sem.at[0]),
        pltpu.make_async_copy(seg, sv, local_sem.at[1]),
        pltpu.make_async_copy(gain, gv, local_sem.at[2]),
        pltpu.make_async_copy(atab, at, local_sem.at[3]),
        pltpu.make_async_copy(ctab, ct, local_sem.at[4]),
        pltpu.make_async_copy(stab, st, local_sem.at[5]),
        pltpu.make_async_copy(wq, w.at[:, pl.ds(0, wide_q)], local_sem.at[6]),
        pltpu.make_async_copy(wk, w.at[:, pl.ds(wide_q, HEAD)], local_sem.at[7]),
        pltpu.make_async_copy(wv, w.at[:, pl.ds(wide_q + HEAD, HEAD)], local_sem.at[8]),
    ]

    barrier = pltpu.get_barrier_semaphore()
    one, zero = jnp.int32(1), jnp.int32(0)
    links = [(c >= d, c - d) for d in DIRECT] + [(c + d <= last, c + d) for d in DIRECT]
    for back, d in EXTRA:
        links.append((c == last - back, c + d))
        links.append((c == last - back + d, c - d))
    for where in (left, right):
        pl.semaphore_signal(barrier, inc=1, device_id={"tensor": where}, device_id_type=MESH)
    expected = jnp.int32(2)
    for cond, where in links:

        @pl.when(cond)
        def _(where=where):
            pl.semaphore_signal(barrier, inc=1, device_id={"context": where}, device_id_type=MESH)

        expected = expected + jnp.where(cond, one, zero)
    for load in loads:
        load.start()
    pl.semaphore_wait(barrier, expected)

    def unit(u):
        return x.at[pl.ds(u * half, half)]

    def ring_copy(k, to_right):
        first = 2 if to_right else 3
        if k < 2:
            src = tok.at[pl.ds((k if to_right else 1 - k) * half, half)]
        else:
            src = unit(first + 2 * (k - 2))
        return pltpu.make_async_remote_copy(
            src_ref=src,
            dst_ref=unit(first + 2 * k),
            send_sem=(rs_send if to_right else ls_send).at[k],
            recv_sem=(rs_recv if to_right else ls_recv).at[k],
            device_id={"tensor": right if to_right else left},
            device_id_type=MESH,
        )

    def ring_step(k):
        for to_right in (True, False):
            ring_copy(k, to_right).wait_recv()
            if k <= 4:
                ring_copy(k + 2, to_right).start()

    def kv_copy(m, src_slot, dst_slot, target, sem):
        return pltpu.make_async_remote_copy(
            src_ref=kv.at[m, pl.ds(src_slot * sub, sub)],
            dst_ref=kv.at[m, pl.ds(dst_slot * sub, sub)],
            send_sem=sem,
            recv_sem=kv_recv.at[dst_slot - 1, m],
            device_id={"context": target},
            device_id_type=MESH,
        )

    def own_copies(m):
        res = [
            (c + d <= last, kv_copy(m, 0, d, c + d, own_sem.at[i, m % 2])) for i, d in enumerate(DIRECT)
        ]
        for back, d in EXTRA:
            res.append((c == last - back, kv_copy(m, 0, d, c + d, own_sem.at[{6: 3, 5: 1}[d], m % 2])))
        return res

    def passed_copies(m, slot):
        first = 0 if slot == 2 else 2
        return [
            (
                (c >= slot) & (c + step <= last),
                kv_copy(m, slot, there, c + step, fwd_sem.at[first + i, m % 2]),
            )
            for i, (step, there) in enumerate(PASSED[slot])
        ]

    def start_all(copies):
        for cond, copy in copies:

            @pl.when(cond)
            def _(copy=copy):
                copy.start()

    def leave_all(copies):
        for cond, copy in copies:

            @pl.when(cond)
            def _(copy=copy):
                copy.wait_send()

    def landed(m, d):
        @pl.when(c >= d)
        def _():
            kv_copy(m, d, d, c, own_sem.at[0, m % 2]).wait_recv()

    def own_send(m):
        if m >= 2:
            leave_all(own_copies(m - 2))
        start_all(own_copies(m))

    def relay(m):
        for slot in PASSED:
            landed(m, slot)
            if m >= 2:
                leave_all(passed_copies(m - 2, slot))
            start_all(passed_copies(m, slot))

    def arrived(m):
        for d in WAITED:
            landed(m, d)

    if RING:
        for k in (0, 1):
            ring_copy(k, True).start()
            ring_copy(k, False).start()

    lane = lax.broadcasted_iota(jnp.int32, (1, HEAD), 1)
    places = [lax.rem(t + o + nten, nten) * sub + h * half for o, h in ARRIVAL]
    for u in range(2 * nten):
        spot = (places[u] + lax.broadcasted_iota(jnp.int32, (half, HEAD), 0)).astype(f32)
        lp[u * half : (u + 1) * half, :] = spot
        for h in range(heads):
            r = (u // 2) * tile + h * sub + (u % 2) * half
            qp[r : r + half, :] = spot
    for i in (1, 3, 4, 5):
        loads[i].wait()
    total_rows = nctx * rows
    segv = sv[...]
    begin = jnp.where(lane >= DOCS, f32(total_rows), f32(0.0))
    end = jnp.full((1, HEAD), total_rows, f32)
    for e in range(1, DOCS):
        count = jnp.sum(jnp.where(segv < e, f32(1.0), f32(0.0)))
        begin = jnp.where(lane == e, count, begin)
        end = jnp.where(lane == e - 1, count, end)
    begin = jnp.where(lane == DOCS, f32(-total_rows), begin)
    end = jnp.where(lane == DOCS, f32(0.0), end)
    missing = jnp.where(lane == DOCS, f32(1.0), f32(0.0)).astype(bf16)
    mine = lax.broadcasted_iota(jnp.int32, (nctx, 2 * HEAD), 0) == c
    both = jnp.sum(jnp.where(mine, at[...], 0.0), 0, keepdims=True)
    ca, sa = both[:, 0:HEAD], both[:, HEAD : 2 * HEAD]
    sign = jnp.where(lane < HEAD // 2, f32(-1.0), f32(1.0))
    for u in range(2 * nten):
        here = pl.ds(pl.multiple_of(places[u], half), half)
        cb, sb = ct[here, :], st[here, :]
        cosv[u * half : (u + 1) * half, :] = ca * cb - sa * sb
        sinv[u * half : (u + 1) * half, :] = (sa * cb + ca * sb) * sign

    def masks(m, carry):
        local = lp[pl.ds(pl.multiple_of(m * sub, sub), sub), :]
        for d in range(slots):
            here = local + ((c - d) * rows).astype(f32)
            kaug[m, d * sub : (d + 1) * sub, :] = jnp.where(
                (here >= begin) & (here < end), f32(1.0), f32(0.0)
            ).astype(bf16)
        kaug[m, slots * sub :, :] = jnp.broadcast_to(missing, (kaug.shape[1] - slots * sub, HEAD))
        kv[m, slots * sub :, :] = jnp.zeros((kv.shape[1] - slots * sub, 2 * HEAD), bf16)
        qaug = jnp.where(kaug[m, 0:sub, :].astype(f32) > 0.5, f32(0.0), f32(NEG)).astype(bf16)
        for h in range(heads):
            r = pl.multiple_of(m * tile + h * sub, sub)
            q[pl.ds(r, sub), HEAD : 2 * HEAD] = qaug
        for d in range(1, slots):

            @pl.when(c < d)
            def _():
                kv[m, d * sub : (d + 1) * sub, :] = jnp.zeros((sub, 2 * HEAD), bf16)

        return carry

    lax.fori_loop(0, msgs, masks, 0)
    for m in range(msgs):
        spot = jnp.where(
            lane < half,
            places[2 * m] + lane,
            jnp.where(lane < sub, places[2 * m + 1] + lane - half, -1),
        ).astype(f32)
        kp[m] = jnp.broadcast_to(spot, (8, HEAD))
    acc[...] = jnp.zeros_like(acc)
    tot[...] = jnp.zeros_like(tot)
    mx[...] = jnp.full_like(mx, LOW)

    scale = math.log2(math.e) / math.sqrt(HEAD)

    def rotate(v, r0):
        here = slice(r0, r0 + sub)
        return v * cosv[here, :] + pltpu.roll(v, HEAD // 2, 1) * sinv[here, :]

    def project_keys(m):
        r0 = m * sub

        def norm(i, carry):
            v = x[pl.ds(r0 + i * 16, 16), :].astype(f32)
            mean = jnp.sum(v * v, -1, keepdims=True) * (1.0 / v.shape[1])
            nrm[pl.ds(i * 16, 16), :] = (v * lax.rsqrt(mean + 1e-05) * gv[...].astype(f32)).astype(
                bf16
            )
            return carry

        lax.fori_loop(0, sub // 16, norm, 0)
        got = jnp.dot(nrm[...], w[:, wide_q:], preferred_element_type=f32)
        kv[m, 0:sub, 0:HEAD] = rotate(got[:, 0:HEAD], r0).astype(bf16)
        kv[m, 0:sub, HEAD : 2 * HEAD] = got[:, HEAD:].astype(bf16)

    def project_queries(m):
        got = jnp.dot(nrm[...], w[:, 0:wide_q], preferred_element_type=f32)
        for h in range(heads):
            r = m * tile + h * sub
            v = rotate(got[:, h * HEAD : (h + 1) * HEAD], m * sub)
            q[r : r + sub, 0:HEAD] = (v * scale).astype(bf16)

    chunks = kv.shape[1] // HEAD

    def attend(lo, hi, *js):
        here = slice(lo * tile, hi * tile)
        queries, spots = q[here, :], qp[here, :]
        cols = []
        for j in js:
            keys = jnp.concatenate([kv[j, :, 0:HEAD], kaug[j]], 1)
            s = lax.dot_general(queries, keys, (((1,), (1,)), ((), ())), preferred_element_type=f32)
            new = [s[:, i * HEAD : (i + 1) * HEAD] for i in range(chunks)]
            new[0] = jnp.where(kp[j][0:1, :] <= spots, new[0], NEG)
            cols.append(new)
        old = mx[here, :]
        top = functools.reduce(jnp.maximum, sum(cols, []))
        new = jnp.maximum(old, jnp.max(top, -1, keepdims=True))
        fade = jnp.exp2(old - new)
        mx[here, :] = new
        whole, got = tot[here, :] * fade, acc[here, :] * fade
        for j, part in zip(js, cols):
            p = [jnp.exp2(v - new) for v in part]
            whole = whole + functools.reduce(jnp.add, p)
            low = jnp.concatenate([v.astype(bf16) for v in p], 1)
            got = got + jnp.dot(low, kv[j, :, HEAD : 2 * HEAD], preferred_element_type=f32)
        tot[here, :] = whole
        acc[here, :] = got

    for i in (0, 2, 6, 7, 8):
        loads[i].wait()
    for s in range(msgs):
        if RING and s >= 1:
            ring_step(s - 1)
        if PROJ:
            project_keys(s)
        if KV:
            own_send(s)
            if s >= 1:
                relay(s - 1)
        if PROJ:
            project_queries(s)
        if KV and s >= 2:
            arrived(s - 2)
        if ATT:
            for job in PLAN.get(s, ()):
                attend(*job)
    for m in (msgs - 2, msgs - 1):
        if KV and m == msgs - 2:
            relay(msgs - 1)
        if KV:
            arrived(m)
        if ATT:
            for job in PLAN[m + 2]:
                attend(*job)

    for i in range(msgs):
        for h in range(heads):
            r = i * tile + h * sub
            whole = jnp.sum(tot[r : r + sub, :], -1, keepdims=True)
            done = (acc[r : r + sub, :] / whole).astype(bf16)
            for u in (0, 1):
                there = pl.ds(pl.multiple_of(places[2 * i + u], half), half)
                out[there, h * HEAD : (h + 1) * HEAD] = done[u * half : (u + 1) * half]

    if RING:
        for k in range(7):
            ring_copy(k, True).wait_send()
            ring_copy(k, False).wait_send()
    if KV:
        for m in (msgs - 2, msgs - 1):
            leave_all(own_copies(m) + passed_copies(m, 2) + passed_copies(m, 7))


def tables(rows, nctx):
    freq = np.exp(-(np.arange(HEAD // 2) * (2.0 / HEAD)) * math.log(500000.0))
    fine = np.arange(rows)[:, None] * freq[None, :]
    coarse = (np.arange(nctx) * rows)[:, None] * freq[None, :]
    twice = lambda v: np.concatenate([v, v], 1).astype(np.float32)
    both = np.concatenate([twice(np.cos(coarse)), twice(np.sin(coarse))], 1)
    return twice(np.cos(fine)), twice(np.sin(fine)), both


def solution(mesh):
    nctx, nten = mesh.shape["context"], mesh.shape["tensor"]

    def body(tokens, norm_gain, w_query, key_matrix, value_matrix, seg_ids):
        sub, width = tokens.shape
        rows = sub * nten
        wide_q = w_query.shape[1]
        heads = wide_q // HEAD
        reach = 4096 // rows
        key_rows = pl.cdiv((reach + 1) * sub, HEAD) * HEAD
        ctab, stab, atab = tables(rows, nctx)

        hbm = pl.BlockSpec(memory_space=pl.ANY)
        dma = pltpu.SemaphoreType.DMA
        f32, bf16 = jnp.float32, jnp.bfloat16
        return pl.pallas_call(
            functools.partial(kernel, sub, reach, nctx, nten),
            out_shape=jax.ShapeDtypeStruct((rows, wide_q), bf16),
            in_specs=[hbm] * 9,
            out_specs=pl.BlockSpec(memory_space=pltpu.VMEM),
            scratch_shapes=[
                pltpu.VMEM((rows, width), bf16),
                pltpu.VMEM((width, wide_q + 2 * HEAD), bf16),
                pltpu.VMEM((sub, width), bf16),
                pltpu.VMEM((heads * rows, 2 * HEAD), bf16),
                pltpu.VMEM((nten, key_rows, 2 * HEAD), bf16),
                pltpu.VMEM((nten, key_rows, HEAD), bf16),
                pltpu.VMEM((rows, HEAD), f32),
                pltpu.VMEM((heads * rows, HEAD), f32),
                pltpu.VMEM((nten, 8, HEAD), f32),
                pltpu.VMEM((rows, HEAD), f32),
                pltpu.VMEM((rows, HEAD), f32),
                pltpu.VMEM((rows, HEAD), f32),
                pltpu.VMEM((rows, HEAD), f32),
                pltpu.VMEM((nctx, 2 * HEAD), f32),
                pltpu.VMEM((1, width), bf16),
                pltpu.VMEM((seg_ids.shape[0] // HEAD, HEAD), jnp.int32),
                pltpu.VMEM((heads * rows, HEAD), f32),
                pltpu.VMEM((heads * rows, HEAD), f32),
                pltpu.VMEM((heads * rows, HEAD), f32),
                dma((9,)),
                dma((7,)),
                dma((7,)),
                dma((7,)),
                dma((7,)),
                dma((4, 2)),
                dma((4, 2)),
                dma((reach, nten)),
            ],
            compiler_params=pltpu.CompilerParams(
                collective_id=0, has_side_effects=True, vmem_limit_bytes=60 << 20
            ),
        )(
            tokens,
            norm_gain.reshape(1, width),
            w_query,
            key_matrix,
            value_matrix,
            seg_ids.reshape(-1, HEAD),
            ctab,
            stab,
            atab,
        )

    in_specs = (
        P(("dp", "context", "tensor"), None),
        P(),
        P(None, "tensor"),
        P(None, "tensor"),
        P(None, "tensor"),
        P("dp"),
    )
    out_specs = P(("dp", "context"), "tensor")
    return jax.shard_map(body, mesh=mesh, in_specs=in_specs, out_specs=out_specs, check_vma=False)
```
